32 devices in a mesh: rows: 8 (over y, x, core), loop: 4 (over z).
Axes of the slice: x: 2, y: 2, z: 4, core: 2. Of those that a mesh axis runs over, the one named last changes fastest.
Arguments:
- integrals: float32 [2, 2, 8192, 8192], P(None, None, 'rows', 'loop'), may hold values from -6 to 6
- mask: int32 [2, 64, 64], P(None, 'rows', 'loop'), may hold values 0 or 1
- coeffs: float32 [8192, 640], P('loop'), may hold values from -0.0625 to 0.0625
Outputs:
- exchange: float32 [8192, 8192], P('rows', 'loop')
The draws below stay inside these ranges and needn't reach their ends.
All inputs are finite; a program needn't handle non-finite values. No bound on the sum of `mask` on one device may be relied on, other than what follows from the above.
Results may differ from the reference program's by a relative error of at most 0.00009.
Values sent between devices are 32-bit elements; how exact they have to be, the bound alone decides.
A program may use at most 192 MiB of HBM per device.

```python
import jax
import jax.numpy as jnp
from jax import lax

NBF = 8192
NOCC = 640
TILE = 128
NSLAB = 2
AUX = 2


def plant(result, key, smallest, largest):
    index_at = [jax.random.randint(jax.random.fold_in(key, axis), (), 0, length) for axis, length in enumerate(result.shape)]
    longest = result.shape.index(max(result.shape))
    next_to = index_at[:longest] + [(index_at[longest] + 1) % result.shape[longest]] + index_at[longest + 1:]
    return result.at[tuple(index_at)].set(smallest).at[tuple(next_to)].set(largest)


def shard_levels(own_key, shape, split, low, largest):
    gain, own = 1.0, jax.random.fold_in(own_key, 6)
    for dim, blocks in split:
        draws = jnp.exp(jax.random.uniform(jax.random.fold_in(own, dim), (blocks,), jnp.float32, low / len(split), largest / len(split)))
        gain = gain * jnp.repeat(draws, shape[dim] // blocks).reshape([-1 if axis == dim else 1 for axis in range(len(shape))])
    return gain


def normal_values(key, extent, width, most, split=(), dtype=jnp.bfloat16):
    result = jax.random.normal(key, extent, jnp.float32) * width
    if len(split) > 0:
        result = shard_levels(key, extent, split, -0.22, 0.18) * result
    return jnp.clip(result, min=-most, max=most).astype(dtype)


def setup_inputs(seed: int = 0) -> dict:
    arg_keys = jax.random.split(jax.random.key(seed), 4)
    integrals = normal_values(arg_keys[0], (NSLAB, AUX, NBF, NBF), 1.0, 6.0, ((2, 8), (3, 4)), jnp.float32)
    mask = plant((jax.random.randint(arg_keys[1], (NSLAB, NBF // TILE, NBF // TILE), 0, 2) < 1).astype(jnp.int32), jax.random.fold_in(arg_keys[1], 1), 0, 1)
    coeffs = normal_values(arg_keys[2], (NBF, NOCC), NBF ** -0.5, 0.0625, ((0, 4),), jnp.float32)
    return {"integrals": integrals, "mask": mask, "coeffs": coeffs}


def reference(integrals, mask, coeffs):
    blocks = mask.astype(jnp.float32)[:, None, :, None, :, None]
    shaped = integrals.reshape(NSLAB, AUX, NBF // TILE, TILE, NBF // TILE, TILE)
    masked = (shaped * blocks).reshape(NSLAB * AUX, NBF, NBF)
    half = jnp.einsum('pml,li->ipm', masked, coeffs, precision=lax.Precision.HIGHEST)
    scale = 1.0 / jnp.sqrt(jnp.float32(NSLAB * AUX * NOCC))
    total = jnp.einsum('ipm,ipn->mn', half, half, precision=lax.Precision.HIGHEST)
    return (total * scale).astype(jnp.float32)
```

```python
import functools

import jax
import jax.numpy as jnp
from jax import lax
from jax.experimental import pallas as pl
from jax.experimental.pallas import tpu as pltpu
from jax.sharding import PartitionSpec as P

TILE = 128
CHUNK = 32
GROUP = 8
HOP = 2
REACH = 2
SLOTS = 8
MESH = pl.DeviceIdType.MESH


def split(x):
    high = x.astype(jnp.bfloat16)
    low = (x - high.astype(jnp.float32)).astype(jnp.bfloat16)
    return high, low


def half_kernel(integrals_ref, mask_ref, high_ref, low_ref, out_ref):
    rows, cols = integrals_ref.shape[2:]
    blocks = integrals_ref[0, 0].reshape(rows // TILE, TILE, cols)
    high, low = split((blocks * mask_ref[0]).reshape(rows, cols))

    def times(a, b):
        return lax.dot_general(
            a, b, (((1,), (1,)), ((), ())), preferred_element_type=jnp.float32
        )

    out_ref[0] = times(high_ref[...], high) + times(high_ref[...], low) + times(low_ref[...], high)


def half_partial(integrals, mask, coeffs):
    nslab, naux, mrows, lcols = integrals.shape
    norbit = coeffs.shape[1]
    turned = coeffs.T
    rounded = lax.reduce_precision(turned, 8, 7)
    high, low = rounded.astype(jnp.bfloat16), (turned - rounded).astype(jnp.bfloat16)
    blocks = jnp.repeat(mask.astype(jnp.float32), TILE, axis=2)[:, :, None, :]
    tm = 256
    out = pl.pallas_call(
        half_kernel,
        grid=(nslab, naux, mrows // tm),
        out_shape=jax.ShapeDtypeStruct((nslab * naux, norbit, mrows), jnp.float32),
        in_specs=[
            pl.BlockSpec((1, 1, tm, lcols), lambda s, a, m: (s, a, m, 0)),
            pl.BlockSpec((1, tm // TILE, 1, lcols), lambda s, a, m: (s, m, 0, 0)),
            pl.BlockSpec((norbit, lcols), lambda s, a, m: (0, 0)),
            pl.BlockSpec((norbit, lcols), lambda s, a, m: (0, 0)),
        ],
        out_specs=pl.BlockSpec((1, norbit, tm), lambda s, a, m: (s * naux + a, 0, m)),
        name="half",
    )(integrals, blocks, high, low)
    return out.reshape(nslab * naux * norbit, mrows)


def ring_place(pair, pairs):
    if pairs == 4:
        return pair + (pair // 2) * (1 - 2 * lax.rem(pair, 2))
    return pair


def exchange_kernel(
    loops, row_count, scale, part_ref, out_ref, own, pin, sin, cols, left,
    own_sem, up_send, up_recv, dn_send, dn_recv, ch_send, ch_recv, pt_send, pt_recv,
):
    depth, mrows = own.shape
    count = depth // CHUNK
    span = CHUNK * GROUP
    pairs = row_count // 2
    r, l = lax.axis_index("rows"), lax.axis_index("loop")
    pair, core = r // 2, lax.rem(r, 2)
    partner = r + 1 - 2 * core
    turn = 1 - 2 * core
    place = ring_place(pair, pairs)
    far = lax.rem((place - ring_place(l, pairs)) * turn + pairs, pairs)
    ahead = ring_place(lax.rem(place + turn + pairs, pairs), pairs) * 2 + core
    behind = ring_place(lax.rem(place - turn + pairs, pairs), pairs) * 2 + core

    load = pltpu.make_async_copy(part_ref, own, own_sem)
    load.start()

    barrier = pltpu.get_barrier_semaphore()
    for other in (partner, ahead, behind):
        pl.semaphore_signal(barrier, inc=1, device_id={"rows": other}, device_id_type=MESH)

    @pl.when(l > 0)
    def _():
        pl.semaphore_signal(barrier, inc=1, device_id={"loop": l - 1}, device_id_type=MESH)

    @pl.when(l < loops - 1)
    def _():
        pl.semaphore_signal(barrier, inc=1, device_id={"loop": l + 1}, device_id_type=MESH)

    neighbours = jnp.where(l > 0, 1, 0) + jnp.where(l < loops - 1, 1, 0)
    pl.semaphore_wait(barrier, 3 + neighbours)

    load.wait()

    def rows_of(j):
        return pl.ds(pl.multiple_of(j * CHUNK, CHUNK), CHUNK)

    def copy(src, dst, send, recv, j, target):
        return pltpu.make_async_remote_copy(
            src_ref=src, dst_ref=dst, send_sem=send.at[lax.rem(j, SLOTS)], recv_sem=recv.at[j],
            device_id=target, device_id_type=MESH,
        )

    def up(j):
        return copy(pin.at[rows_of(j)], pin.at[rows_of(j)], up_send, up_recv, j, {"loop": l + 1})

    def down(j):
        return copy(sin.at[rows_of(j)], sin.at[rows_of(j)], dn_send, dn_recv, j, {"loop": l - 1})

    def chain(j):
        ref = cols.at[core, rows_of(j)]
        return copy(ref, ref, ch_send, ch_recv, j, {"rows": ahead})

    def share(j):
        ref = cols.at[core, rows_of(j)]
        return copy(ref, ref, pt_send, pt_recv, j, {"rows": partner})

    def taken(j):
        ref = cols.at[1 - core, rows_of(j)]
        return copy(ref, ref, pt_send, pt_recv, j, {"rows": partner})

    def send(make, j):
        @pl.when(j >= SLOTS)
        def _():
            make(j - SLOTS).wait_send()

        make(j).start()

    def line(held, make, j, first, last):
        @pl.when((j >= 0) & (j < count))
        def _():
            at = rows_of(j)

            @pl.when(first)
            def _():
                held[at, :] = own[at, :]

            @pl.when(jnp.logical_not(first))
            def _():
                make(j).wait_recv()
                held[at, :] = held[at, :] + own[at, :]

            @pl.when(jnp.logical_not(last))
            def _():
                send(make, j)

    settle = HOP * jnp.maximum(l, loops - 1 - l)

    def multiply(g):
        at = pl.ds(pl.multiple_of(g * span, span), span)

        @pl.loop(0, mrows // 256)
        def _(m):
            mine = pl.ds(pl.multiple_of(m * 256, 256), 256)
            high, low = split(own[at, mine].T)
            left[mine, pl.ds(0, span)] = high
            left[mine, pl.ds(span, span)] = high
            left[mine, pl.ds(2 * span, span)] = low

        for block in range(2):

            @pl.loop(0, mrows // 256)
            def _(n):
                high, low = split(cols[block, at, pl.ds(pl.multiple_of(n * 256, 256), 256)])
                right = jnp.concatenate([high, low, high], axis=0)
                theirs = pl.ds(pl.multiple_of(block * mrows + n * 256, 256), 256)

                @pl.loop(0, mrows // 256)
                def _(m):
                    mine = pl.ds(pl.multiple_of(m * 256, 256), 256)
                    part = jnp.dot(left[mine, :], right, preferred_element_type=jnp.float32) * scale

                    @pl.when(g == 0)
                    def _():
                        out_ref[mine, theirs] = part

                    @pl.when(g > 0)
                    def _():
                        out_ref[mine, theirs] = out_ref[mine, theirs] + part

    def step(t, carry):
        line(pin, up, t - HOP * l, l == 0, l == loops - 1)
        line(sin, down, t - HOP * (loops - 1 - l), l == loops - 1, l == 0)

        done = t - settle

        @pl.when((done >= 0) & (done < count))
        def _():
            at = rows_of(done)
            total = pin[at, :] + (sin[at, :] - own[at, :])
            own[at, :] = total

            @pl.when(far == 0)
            def _():
                cols[core, at, :] = total

        passed = done - REACH * far

        @pl.when((passed >= 0) & (passed < count))
        def _():
            @pl.when(far > 0)
            def _():
                chain(passed).wait_recv()

            @pl.when(far < pairs - 1)
            def _():
                send(chain, passed)

            send(share, passed)

        ready = done - REACH * pairs

        @pl.when((ready >= 0) & (ready < count))
        def _():
            taken(ready).wait_recv()

            @pl.when(lax.rem(ready, GROUP) == GROUP - 1)
            def _():
                multiply(ready // GROUP)

        return carry

    lax.fori_loop(0, count + HOP * (loops - 1) + REACH * pairs, step, 0)

    def drain(i, carry):
        j = count - SLOTS + i

        @pl.when(l < loops - 1)
        def _():
            up(j).wait_send()

        @pl.when(l > 0)
        def _():
            down(j).wait_send()

        @pl.when(far < pairs - 1)
        def _():
            chain(j).wait_send()

        share(j).wait_send()
        return carry

    lax.fori_loop(0, SLOTS, drain, 0)


def local(loops, row_count, integrals, mask, coeffs):
    mrows, lcols = integrals.shape[2:]
    part = half_partial(integrals, mask, coeffs)
    depth = part.shape[0]
    assert lcols == 2 * mrows and row_count == 2 * loops
    count = depth // CHUNK
    assert depth % (CHUNK * GROUP) == 0
    dma = pltpu.SemaphoreType.DMA
    return pl.pallas_call(
        functools.partial(exchange_kernel, loops, row_count, float(depth) ** -0.5),
        out_shape=jax.ShapeDtypeStruct((mrows, lcols), jnp.float32),
        in_specs=[pl.BlockSpec(memory_space=pl.ANY)],
        out_specs=pl.BlockSpec(memory_space=pltpu.VMEM),
        scratch_shapes=[
            pltpu.VMEM((depth, mrows), jnp.float32),
            pltpu.VMEM((depth, mrows), jnp.float32),
            pltpu.VMEM((depth, mrows), jnp.float32),
            pltpu.VMEM((2, depth, mrows), jnp.float32),
            pltpu.VMEM((mrows, 3 * CHUNK * GROUP), jnp.bfloat16),
            dma,
        ]
        + [dma((SLOTS,)), dma((count,))] * 4,
        compiler_params=pltpu.CompilerParams(
            collective_id=0, has_side_effects=True, vmem_limit_bytes=67043328
        ),
        name="exchange",
    )(part)


def solution(mesh):
    in_specs = (P(None, None, "rows", "loop"), P(None, "rows", "loop"), P("loop", None))
    out_specs = P("rows", "loop")
    body = functools.partial(local, mesh.shape["loop"], mesh.shape["rows"])
    return jax.shard_map(body, mesh=mesh, in_specs=in_specs, out_specs=out_specs, check_vma=False)
```

```python
import functools

import jax
import jax.numpy as jnp
from jax import lax
from jax.experimental import pallas as pl
from jax.experimental.pallas import tpu as pltpu
from jax.sharding import PartitionSpec as P

TILE = 128
CHUNK = 32
GROUP = 8
HOP = 2
REACH = 2
SLOTS = 8
MESH = pl.DeviceIdType.MESH


def split(x):
    high = x.astype(jnp.bfloat16)
    low = (x - high.astype(jnp.float32)).astype(jnp.bfloat16)
    return high, low


def ring_place(pair, pairs):
    if pairs == 4:
        return pair + (pair // 2) * (1 - 2 * lax.rem(pair, 2))
    return pair


def exchange_kernel(
    loops, row_count, scale, integrals_ref, mask_ref, coeffs_ref, out_ref,
    own, pin, sin, cols, left, high_ref, low_ref, tile, spare, tile_sem, coeffs_sem,
    up_send, up_recv, dn_send, dn_recv, ch_send, ch_recv, pt_send, pt_recv,
):
    depth, mrows = own.shape
    naux, lcols = integrals_ref.shape[1], integrals_ref.shape[3]
    norbit = coeffs_ref.shape[1]
    ring = pin.shape[0] // CHUNK
    wide = tile.shape[1]
    tiles = mrows // wide
    tile_count = integrals_ref.shape[0] * naux * tiles
    count = depth // CHUNK
    span = CHUNK * GROUP
    pairs = row_count // 2
    r, l = lax.axis_index("rows"), lax.axis_index("loop")
    pair, core = r // 2, lax.rem(r, 2)
    partner = r + 1 - 2 * core
    turn = 1 - 2 * core
    place = ring_place(pair, pairs)
    far = lax.rem((place - ring_place(l, pairs)) * turn + pairs, pairs)
    ahead = ring_place(lax.rem(place + turn + pairs, pairs), pairs) * 2 + core
    behind = ring_place(lax.rem(place - turn + pairs, pairs), pairs) * 2 + core

    def fetch(u):
        part, m = u // tiles, lax.rem(u, tiles)
        return pltpu.make_async_copy(
            integrals_ref.at[
                part // naux, lax.rem(part, naux), pl.ds(pl.multiple_of(m * wide, wide), wide), :
            ],
            tile.at[lax.rem(u, 2)],
            tile_sem.at[lax.rem(u, 2)],
        )

    def half(u):
        part, m = u // tiles, lax.rem(u, tiles)
        fetch(u).wait()
        blocks = tile[lax.rem(u, 2)].reshape(wide // TILE, TILE, lcols)
        mask = mask_ref[part // naux, m][:, None, :]
        high, low = split((blocks * mask).reshape(wide, lcols))

        def times(a, b):
            return lax.dot_general(
                a, b, (((1,), (1,)), ((), ())), preferred_element_type=jnp.float32
            )

        value = times(high_ref[...], high) + times(high_ref[...], low) + times(low_ref[...], high)
        at = pl.ds(pl.multiple_of(part * norbit, norbit), norbit)
        own[at, pl.ds(pl.multiple_of(m * wide, wide), wide)] = value

        @pl.when(u + 2 < tile_count)
        def _():
            fetch(u + 2).start()

    room = spare if spare.shape == coeffs_ref.shape else cols.at[0, pl.ds(0, lcols), pl.ds(0, norbit)]
    load = pltpu.make_async_copy(coeffs_ref, room, coeffs_sem)
    load.start()
    fetch(0).start()
    fetch(1).start()
    load.wait()

    @pl.loop(0, lcols // 256)
    def _(n):
        at = pl.ds(pl.multiple_of(n * 256, 256), 256)
        high_ref[:, at], low_ref[:, at] = split(room[at, :].T)

    barrier = pltpu.get_barrier_semaphore()
    for other in (partner, ahead, behind):
        pl.semaphore_signal(barrier, inc=1, device_id={"rows": other}, device_id_type=MESH)

    @pl.when(l > 0)
    def _():
        pl.semaphore_signal(barrier, inc=1, device_id={"loop": l - 1}, device_id_type=MESH)

    @pl.when(l < loops - 1)
    def _():
        pl.semaphore_signal(barrier, inc=1, device_id={"loop": l + 1}, device_id_type=MESH)

    neighbours = jnp.where(l > 0, 1, 0) + jnp.where(l < loops - 1, 1, 0)
    pl.semaphore_wait(barrier, 3 + neighbours)

    @pl.loop(0, tiles)
    def _(u):
        half(u)

    pace = max(norbit // CHUNK // tiles, 1)

    def rows_of(j):
        return pl.ds(pl.multiple_of(j * CHUNK, CHUNK), CHUNK)

    def slot_of(j):
        return pl.ds(pl.multiple_of(lax.rem(j, ring) * CHUNK, CHUNK), CHUNK)

    def copy(src, dst, send, recv, j, target):
        return pltpu.make_async_remote_copy(
            src_ref=src, dst_ref=dst, send_sem=send.at[lax.rem(j, SLOTS)], recv_sem=recv.at[j],
            device_id=target, device_id_type=MESH,
        )

    def up(j):
        return copy(pin.at[slot_of(j)], pin.at[slot_of(j)], up_send, up_recv, j, {"loop": l + 1})

    def down(j):
        return copy(sin.at[slot_of(j)], sin.at[slot_of(j)], dn_send, dn_recv, j, {"loop": l - 1})

    def chain(j):
        ref = cols.at[core, rows_of(j)]
        return copy(ref, ref, ch_send, ch_recv, j, {"rows": ahead})

    def share(j):
        ref = cols.at[core, rows_of(j)]
        return copy(ref, ref, pt_send, pt_recv, j, {"rows": partner})

    def taken(j):
        ref = cols.at[1 - core, rows_of(j)]
        return copy(ref, ref, pt_send, pt_recv, j, {"rows": partner})

    def send(make, j):
        @pl.when(j >= SLOTS)
        def _():
            make(j - SLOTS).wait_send()

        make(j).start()

    def line(held, make, j, first, last):
        @pl.when((j >= 0) & (j < count))
        def _():
            at, slot = rows_of(j), slot_of(j)

            @pl.when(first)
            def _():
                held[slot, :] = own[at, :]

            @pl.when(jnp.logical_not(first))
            def _():
                make(j).wait_recv()
                held[slot, :] = held[slot, :] + own[at, :]

            @pl.when(jnp.logical_not(last))
            def _():
                send(make, j)

    settle = HOP * jnp.maximum(l, loops - 1 - l)

    def multiply(g, n):
        at = pl.ds(pl.multiple_of(g * span, span), span)

        @pl.when(n == 0)
        def _():
            @pl.loop(0, mrows // 256)
            def _(m):
                mine = pl.ds(pl.multiple_of(m * 256, 256), 256)
                high, low = split(own[at, mine].T)
                left[mine, pl.ds(0, span)] = high
                left[mine, pl.ds(span, span)] = high
                left[mine, pl.ds(2 * span, span)] = low

        @pl.when(n < 2 * (mrows // 256))
        def _():
            block = n // (mrows // 256)
            inner = pl.multiple_of(lax.rem(n, mrows // 256) * 256, 256)
            high, low = split(cols[block, at, pl.ds(inner, 256)])
            right = jnp.concatenate([high, low, high], axis=0)
            theirs = pl.ds(pl.multiple_of(n * 256, 256), 256)

            @pl.loop(0, mrows // 256)
            def _(m):
                mine = pl.ds(pl.multiple_of(m * 256, 256), 256)
                part = jnp.dot(left[mine, :], right, preferred_element_type=jnp.float32) * scale

                @pl.when(g == 0)
                def _():
                    out_ref[mine, theirs] = part

                @pl.when(g > 0)
                def _():
                    out_ref[mine, theirs] = out_ref[mine, theirs] + part

    def step(t, carry):
        line(pin, up, t - HOP * l, l == 0, l == loops - 1)
        line(sin, down, t - HOP * (loops - 1 - l), l == loops - 1, l == 0)

        done = t - settle

        @pl.when((done >= 0) & (done < count))
        def _():
            at, slot = rows_of(done), slot_of(done)
            total = pin[slot, :] + (sin[slot, :] - own[at, :])
            own[at, :] = total

            @pl.when(far == 0)
            def _():
                cols[core, at, :] = total

        passed = done - REACH * far

        @pl.when((passed >= 0) & (passed < count))
        def _():
            @pl.when(far > 0)
            def _():
                chain(passed).wait_recv()

            @pl.when(far < pairs - 1)
            def _():
                send(chain, passed)

            send(share, passed)

        ready = done - REACH * pairs

        @pl.when((ready >= 0) & (ready < count))
        def _():
            taken(ready).wait_recv()

        @pl.when((ready >= GROUP) & (ready < count + GROUP))
        def _():
            multiply(ready // GROUP - 1, lax.rem(ready, GROUP))

        later = tiles + t // pace

        @pl.when((lax.rem(t, pace) == pace // 2) & (later < tile_count))
        def _():
            half(later)

        return carry

    lax.fori_loop(0, count + HOP * (loops - 1) + REACH * pairs + GROUP, step, 0)

    def drain(i, carry):
        j = count - SLOTS + i

        @pl.when(l < loops - 1)
        def _():
            up(j).wait_send()

        @pl.when(l > 0)
        def _():
            down(j).wait_send()

        @pl.when(far < pairs - 1)
        def _():
            chain(j).wait_send()

        share(j).wait_send()
        return carry

    lax.fori_loop(0, SLOTS, drain, 0)


def local(loops, row_count, integrals, mask, coeffs):
    nslab, naux, mrows, lcols = integrals.shape
    norbit = coeffs.shape[1]
    depth = nslab * naux * norbit
    count = depth // CHUNK
    wide = 2 * TILE
    assert lcols == 2 * mrows and row_count == 2 * loops and norbit % CHUNK == 0
    assert depth % (CHUNK * GROUP) == 0 and 2 * mrows // 256 <= GROUP
    ring = min(count, SLOTS + 3 * HOP * loops)
    spare = (8, 128) if lcols <= depth and norbit <= mrows else (lcols, norbit)
    blocks = jnp.repeat(mask.astype(jnp.float32), TILE, axis=2)
    blocks = blocks.reshape(nslab, mrows // wide, wide // TILE, lcols)
    dma = pltpu.SemaphoreType.DMA
    return pl.pallas_call(
        functools.partial(exchange_kernel, loops, row_count, float(depth) ** -0.5),
        out_shape=jax.ShapeDtypeStruct((mrows, lcols), jnp.float32),
        in_specs=[
            pl.BlockSpec(memory_space=pl.ANY),
            pl.BlockSpec(memory_space=pltpu.VMEM),
            pl.BlockSpec(memory_space=pl.ANY),
        ],
        out_specs=pl.BlockSpec(memory_space=pltpu.VMEM),
        scratch_shapes=[
            pltpu.VMEM((depth, mrows), jnp.float32),
            pltpu.VMEM((ring * CHUNK, mrows), jnp.float32),
            pltpu.VMEM((ring * CHUNK, mrows), jnp.float32),
            pltpu.VMEM((2, depth, mrows), jnp.float32),
            pltpu.VMEM((mrows, 3 * CHUNK * GROUP), jnp.bfloat16),
            pltpu.VMEM((norbit, lcols), jnp.bfloat16),
            pltpu.VMEM((norbit, lcols), jnp.bfloat16),
            pltpu.VMEM((2, wide, lcols), jnp.float32),
            pltpu.VMEM(spare, jnp.float32),
            dma((2,)),
            dma,
        ]
        + [dma((SLOTS,)), dma((count,))] * 4,
        compiler_params=pltpu.CompilerParams(
            collective_id=0, has_side_effects=True, vmem_limit_bytes=67043328
        ),
        name="exchange",
    )(integrals, blocks, coeffs)


def solution(mesh):
    in_specs = (P(None, None, "rows", "loop"), P(None, "rows", "loop"), P("loop", None))
    out_specs = P("rows", "loop")
    body = functools.partial(local, mesh.shape["loop"], mesh.shape["rows"])
    return jax.shard_map(body, mesh=mesh, in_specs=in_specs, out_specs=out_specs, check_vma=False)
```

```python
import functools

import jax
import jax.numpy as jnp
from jax import lax
from jax.experimental import pallas as pl
from jax.experimental.pallas import tpu as pltpu
from jax.sharding import PartitionSpec as P

TILE = 128
CHUNK = 16
GROUP = 16
HOP = 3
REACH = 2
SLOTS = 16
MESH = pl.DeviceIdType.MESH


def split(x):
    high = x.astype(jnp.bfloat16)
    low = (x - high.astype(jnp.float32)).astype(jnp.bfloat16)
    return high, low


def ring_place(pair, pairs):
    if pairs == 4:
        return pair + (pair // 2) * (1 - 2 * lax.rem(pair, 2))
    return pair


def exchange_kernel(
    loops, row_count, scale, integrals_ref, mask_ref, coeffs_ref, out_ref,
    own, pin, sin, cols, left, high_ref, low_ref, tile, spare, tile_sem, coeffs_sem,
    up_send, up_recv, dn_send, dn_recv, ch_send, ch_recv, pt_send, pt_recv,
):
    depth, mrows = own.shape
    naux, lcols = integrals_ref.shape[1], integrals_ref.shape[3]
    norbit = coeffs_ref.shape[1]
    ring = pin.shape[0] // CHUNK
    wide = tile.shape[1]
    tiles = mrows // wide
    tile_count = integrals_ref.shape[0] * naux * tiles
    count = depth // CHUNK
    span = CHUNK * GROUP
    pairs = row_count // 2
    r, l = lax.axis_index("rows"), lax.axis_index("loop")
    pair, core = r // 2, lax.rem(r, 2)
    partner = r + 1 - 2 * core
    turn = 1 - 2 * core
    place = ring_place(pair, pairs)
    far = lax.rem((place - ring_place(l, pairs)) * turn + pairs, pairs)
    ahead = ring_place(lax.rem(place + turn + pairs, pairs), pairs) * 2 + core
    behind = ring_place(lax.rem(place - turn + pairs, pairs), pairs) * 2 + core

    def fetch(u):
        part, m = u // tiles, lax.rem(u, tiles)
        return pltpu.make_async_copy(
            integrals_ref.at[
                part // naux, lax.rem(part, naux), pl.ds(pl.multiple_of(m * wide, wide), wide), :
            ],
            tile.at[lax.rem(u, 2)],
            tile_sem.at[lax.rem(u, 2)],
        )

    def half(u):
        part, m = u // tiles, lax.rem(u, tiles)
        fetch(u).wait()
        blocks = tile[lax.rem(u, 2)].reshape(wide // TILE, TILE, lcols)
        mask = mask_ref[part // naux, m][:, None, :]
        high, low = split((blocks * mask).reshape(wide, lcols))

        def times(a, b):
            return lax.dot_general(
                a, b, (((1,), (1,)), ((), ())), preferred_element_type=jnp.float32
            )

        value = times(high_ref[...], high) + times(high_ref[...], low) + times(low_ref[...], high)
        at = pl.ds(pl.multiple_of(part * norbit, norbit), norbit)
        own[at, pl.ds(pl.multiple_of(m * wide, wide), wide)] = value

        @pl.when(u + 2 < tile_count)
        def _():
            fetch(u + 2).start()

    room = spare if spare.shape == coeffs_ref.shape else cols.at[0, pl.ds(0, lcols), pl.ds(0, norbit)]
    load = pltpu.make_async_copy(coeffs_ref, room, coeffs_sem)
    load.start()
    fetch(0).start()
    fetch(1).start()
    load.wait()

    @pl.loop(0, lcols // 256)
    def _(n):
        at = pl.ds(pl.multiple_of(n * 256, 256), 256)
        high_ref[:, at], low_ref[:, at] = split(room[at, :].T)

    barrier = pltpu.get_barrier_semaphore()
    for other in (partner, ahead, behind):
        pl.semaphore_signal(barrier, inc=1, device_id={"rows": other}, device_id_type=MESH)

    @pl.when(l > 0)
    def _():
        pl.semaphore_signal(barrier, inc=1, device_id={"loop": l - 1}, device_id_type=MESH)

    @pl.when(l < loops - 1)
    def _():
        pl.semaphore_signal(barrier, inc=1, device_id={"loop": l + 1}, device_id_type=MESH)

    neighbours = jnp.where(l > 0, 1, 0) + jnp.where(l < loops - 1, 1, 0)
    pl.semaphore_wait(barrier, 3 + neighbours)

    @pl.loop(0, tiles)
    def _(u):
        half(u)

    pace = max(norbit // CHUNK // tiles, 1)

    def rows_of(j):
        return pl.ds(pl.multiple_of(j * CHUNK, CHUNK), CHUNK)

    def slot_of(j):
        return pl.ds(pl.multiple_of(lax.rem(j, ring) * CHUNK, CHUNK), CHUNK)

    def copy(src, dst, send, recv, j, target):
        return pltpu.make_async_remote_copy(
            src_ref=src, dst_ref=dst, send_sem=send.at[lax.rem(j, SLOTS)], recv_sem=recv.at[j],
            device_id=target, device_id_type=MESH,
        )

    def up(j):
        return copy(pin.at[slot_of(j)], pin.at[slot_of(j)], up_send, up_recv, j, {"loop": l + 1})

    def down(j):
        return copy(sin.at[slot_of(j)], sin.at[slot_of(j)], dn_send, dn_recv, j, {"loop": l - 1})

    def chain(j):
        ref = cols.at[core, rows_of(j)]
        return copy(ref, ref, ch_send, ch_recv, j, {"rows": ahead})

    def share(j):
        ref = cols.at[core, rows_of(j)]
        return copy(ref, ref, pt_send, pt_recv, j, {"rows": partner})

    def taken(j):
        ref = cols.at[1 - core, rows_of(j)]
        return copy(ref, ref, pt_send, pt_recv, j, {"rows": partner})

    def send(make, j):
        @pl.when(j >= SLOTS)
        def _():
            make(j - SLOTS).wait_send()

        make(j).start()

    def line(held, make, j, first, last):
        @pl.when((j >= 0) & (j < count))
        def _():
            at, slot = rows_of(j), slot_of(j)

            @pl.when(first)
            def _():
                held[slot, :] = own[at, :]

            @pl.when(jnp.logical_not(first))
            def _():
                make(j).wait_recv()
                held[slot, :] = held[slot, :] + own[at, :]

            @pl.when(jnp.logical_not(last))
            def _():
                send(make, j)

    settle = HOP * jnp.maximum(l, loops - 1 - l)

    def multiply(g, n):
        at = pl.ds(pl.multiple_of(g * span, span), span)

        @pl.when(n == 0)
        def _():
            @pl.loop(0, mrows // 256)
            def _(m):
                mine = pl.ds(pl.multiple_of(m * 256, 256), 256)
                high, low = split(own[at, mine].T)
                left[mine, pl.ds(0, span)] = high
                left[mine, pl.ds(span, span)] = high
                left[mine, pl.ds(2 * span, span)] = low

        @pl.when(n < 2 * (mrows // 256))
        def _():
            block = n // (mrows // 256)
            inner = pl.multiple_of(lax.rem(n, mrows // 256) * 256, 256)
            high, low = split(cols[block, at, pl.ds(inner, 256)])
            right = jnp.concatenate([high, low, high], axis=0)
            theirs = pl.ds(pl.multiple_of(n * 256, 256), 256)

            @pl.loop(0, mrows // 256)
            def _(m):
                mine = pl.ds(pl.multiple_of(m * 256, 256), 256)
                part = jnp.dot(left[mine, :], right, preferred_element_type=jnp.float32) * scale

                @pl.when(g == 0)
                def _():
                    out_ref[mine, theirs] = part

                @pl.when(g > 0)
                def _():
                    out_ref[mine, theirs] = out_ref[mine, theirs] + part

    def step(t, carry):
        line(pin, up, t - HOP * l, l == 0, l == loops - 1)
        line(sin, down, t - HOP * (loops - 1 - l), l == loops - 1, l == 0)

        done = t - settle

        @pl.when((done >= 0) & (done < count))
        def _():
            at, slot = rows_of(done), slot_of(done)
            total = pin[slot, :] + (sin[slot, :] - own[at, :])
            own[at, :] = total

            @pl.when(far == 0)
            def _():
                cols[core, at, :] = total

        passed = done - REACH * far

        @pl.when((passed >= 0) & (passed < count))
        def _():
            @pl.when(far > 0)
            def _():
                chain(passed).wait_recv()

            @pl.when(far < pairs - 1)
            def _():
                send(chain, passed)

            send(share, passed)

        ready = done - REACH * pairs

        @pl.when((ready >= 0) & (ready < count))
        def _():
            taken(ready).wait_recv()

        @pl.when((ready >= GROUP) & (ready < count + GROUP))
        def _():
            multiply(ready // GROUP - 1, lax.rem(ready, GROUP))

        later = tiles + t // pace

        @pl.when((lax.rem(t, pace) == pace // 2) & (later < tile_count))
        def _():
            half(later)

        return carry

    lax.fori_loop(0, count + HOP * (loops - 1) + REACH * pairs + GROUP, step, 0)

    def drain(i, carry):
        j = count - SLOTS + i

        @pl.when(l < loops - 1)
        def _():
            up(j).wait_send()

        @pl.when(l > 0)
        def _():
            down(j).wait_send()

        @pl.when(far < pairs - 1)
        def _():
            chain(j).wait_send()

        share(j).wait_send()
        return carry

    lax.fori_loop(0, SLOTS, drain, 0)


def local(loops, row_count, integrals, mask, coeffs):
    nslab, naux, mrows, lcols = integrals.shape
    norbit = coeffs.shape[1]
    depth = nslab * naux * norbit
    count = depth // CHUNK
    wide = 2 * TILE
    assert lcols == 2 * mrows and row_count == 2 * loops and norbit % CHUNK == 0
    assert depth % (CHUNK * GROUP) == 0 and 2 * mrows // 256 <= GROUP
    ring = min(count, SLOTS + 3 * HOP * loops)
    spare = (8, 128) if lcols <= depth and norbit <= mrows else (lcols, norbit)
    blocks = jnp.repeat(mask.astype(jnp.float32), TILE, axis=2)
    blocks = blocks.reshape(nslab, mrows // wide, wide // TILE, lcols)
    dma = pltpu.SemaphoreType.DMA
    return pl.pallas_call(
        functools.partial(exchange_kernel, loops, row_count, float(depth) ** -0.5),
        out_shape=jax.ShapeDtypeStruct((mrows, lcols), jnp.float32),
        in_specs=[
            pl.BlockSpec(memory_space=pl.ANY),
            pl.BlockSpec(memory_space=pltpu.VMEM),
            pl.BlockSpec(memory_space=pl.ANY),
        ],
        out_specs=pl.BlockSpec(memory_space=pltpu.VMEM),
        scratch_shapes=[
            pltpu.VMEM((depth, mrows), jnp.float32),
            pltpu.VMEM((ring * CHUNK, mrows), jnp.float32),
            pltpu.VMEM((ring * CHUNK, mrows), jnp.float32),
            pltpu.VMEM((2, depth, mrows), jnp.float32),
            pltpu.VMEM((mrows, 3 * CHUNK * GROUP), jnp.bfloat16),
            pltpu.VMEM((norbit, lcols), jnp.bfloat16),
            pltpu.VMEM((norbit, lcols), jnp.bfloat16),
            pltpu.VMEM((2, wide, lcols), jnp.float32),
            pltpu.VMEM(spare, jnp.float32),
            dma((2,)),
            dma,
        ]
        + [dma((SLOTS,)), dma((count,))] * 4,
        compiler_params=pltpu.CompilerParams(
            collective_id=0, has_side_effects=True, vmem_limit_bytes=67043328
        ),
        name="exchange",
    )(integrals, blocks, coeffs)


def solution(mesh):
    in_specs = (P(None, None, "rows", "loop"), P(None, "rows", "loop"), P("loop", None))
    out_specs = P("rows", "loop")
    body = functools.partial(local, mesh.shape["loop"], mesh.shape["rows"])
    return jax.shard_map(body, mesh=mesh, in_specs=in_specs, out_specs=out_specs, check_vma=False)
```

```python
import functools

import jax
import jax.numpy as jnp
from jax import lax
from jax.experimental import pallas as pl
from jax.experimental.pallas import tpu as pltpu
from jax.sharding import PartitionSpec as P

TILE = 128
CHUNK = 32
GROUP = 8
HOP = 2
REACH = 1
SLOTS = 8
MESH = pl.DeviceIdType.MESH


def split(x):
    high = x.astype(jnp.bfloat16)
    low = (x - high.astype(jnp.float32)).astype(jnp.bfloat16)
    return high, low


def ring_place(pair, pairs):
    if pairs == 4:
        return pair + (pair // 2) * (1 - 2 * lax.rem(pair, 2))
    return pair


def exchange_kernel(
    loops, row_count, scale, integrals_ref, mask_ref, coeffs_ref, out_ref,
    own, pin, sin, cols, left, high_ref, low_ref, tile, spare, tile_sem, coeffs_sem,
    up_send, up_recv, dn_send, dn_recv, ch_send, ch_recv, pt_send, pt_recv,
):
    depth, mrows = own.shape
    naux, lcols = integrals_ref.shape[1], integrals_ref.shape[3]
    norbit = coeffs_ref.shape[1]
    ring = pin.shape[0] // CHUNK
    wide = tile.shape[1]
    tiles = mrows // wide
    tile_count = integrals_ref.shape[0] * naux * tiles
    count = depth // CHUNK
    span = CHUNK * GROUP
    pairs = row_count // 2
    r, l = lax.axis_index("rows"), lax.axis_index("loop")
    pair, core = r // 2, lax.rem(r, 2)
    partner = r + 1 - 2 * core
    turn = 1 - 2 * core
    place = ring_place(pair, pairs)
    far = lax.rem((place - ring_place(l, pairs)) * turn + pairs, pairs)
    ahead = ring_place(lax.rem(place + turn + pairs, pairs), pairs) * 2 + core
    behind = ring_place(lax.rem(place - turn + pairs, pairs), pairs) * 2 + core

    def fetch(u):
        part, m = u // tiles, lax.rem(u, tiles)
        return pltpu.make_async_copy(
            integrals_ref.at[
                part // naux, lax.rem(part, naux), pl.ds(pl.multiple_of(m * wide, wide), wide), :
            ],
            tile.at[lax.rem(u, 2)],
            tile_sem.at[lax.rem(u, 2)],
        )

    def half(u):
        part, m = u // tiles, lax.rem(u, tiles)
        fetch(u).wait()
        blocks = tile[lax.rem(u, 2)].reshape(wide // TILE, TILE, lcols)
        mask = mask_ref[part // naux, m][:, None, :]
        high, low = split((blocks * mask).reshape(wide, lcols))

        def times(a, b):
            return lax.dot_general(
                a, b, (((1,), (1,)), ((), ())), preferred_element_type=jnp.float32
            )

        value = times(high_ref[...], high) + times(high_ref[...], low) + times(low_ref[...], high)
        at = pl.ds(pl.multiple_of(part * norbit, norbit), norbit)
        own[at, pl.ds(pl.multiple_of(m * wide, wide), wide)] = value

        @pl.when(u + 2 < tile_count)
        def _():
            fetch(u + 2).start()

    room = spare if spare.shape == coeffs_ref.shape else cols.at[0, pl.ds(0, lcols), pl.ds(0, norbit)]
    load = pltpu.make_async_copy(coeffs_ref, room, coeffs_sem)
    load.start()
    fetch(0).start()
    fetch(1).start()
    load.wait()

    @pl.loop(0, lcols // 256)
    def _(n):
        at = pl.ds(pl.multiple_of(n * 256, 256), 256)
        high_ref[:, at], low_ref[:, at] = split(room[at, :].T)

    barrier = pltpu.get_barrier_semaphore()
    for other in (partner, ahead, behind):
        pl.semaphore_signal(barrier, inc=1, device_id={"rows": other}, device_id_type=MESH)

    @pl.when(l > 0)
    def _():
        pl.semaphore_signal(barrier, inc=1, device_id={"loop": l - 1}, device_id_type=MESH)

    @pl.when(l < loops - 1)
    def _():
        pl.semaphore_signal(barrier, inc=1, device_id={"loop": l + 1}, device_id_type=MESH)

    neighbours = jnp.where(l > 0, 1, 0) + jnp.where(l < loops - 1, 1, 0)
    pl.semaphore_wait(barrier, 3 + neighbours)

    @pl.loop(0, tiles)
    def _(u):
        half(u)

    pace = max(norbit // CHUNK // tiles, 1)

    def rows_of(j):
        return pl.ds(pl.multiple_of(j * CHUNK, CHUNK), CHUNK)

    def slot_of(j):
        return pl.ds(pl.multiple_of(lax.rem(j, ring) * CHUNK, CHUNK), CHUNK)

    def copy(src, dst, send, recv, j, target):
        return pltpu.make_async_remote_copy(
            src_ref=src, dst_ref=dst, send_sem=send.at[lax.rem(j, SLOTS)], recv_sem=recv.at[j],
            device_id=target, device_id_type=MESH,
        )

    def up(j):
        return copy(pin.at[slot_of(j)], pin.at[slot_of(j)], up_send, up_recv, j, {"loop": l + 1})

    def down(j):
        return copy(sin.at[slot_of(j)], sin.at[slot_of(j)], dn_send, dn_recv, j, {"loop": l - 1})

    def chain(j):
        ref = cols.at[core, rows_of(j)]
        return copy(ref, ref, ch_send, ch_recv, j, {"rows": ahead})

    def share(j):
        ref = cols.at[core, rows_of(j)]
        return copy(ref, ref, pt_send, pt_recv, j, {"rows": partner})

    def taken(j):
        ref = cols.at[1 - core, rows_of(j)]
        return copy(ref, ref, pt_send, pt_recv, j, {"rows": partner})

    def send(make, j):
        @pl.when(j >= SLOTS)
        def _():
            make(j - SLOTS).wait_send()

        make(j).start()

    def line(held, make, j, first, last):
        @pl.when((j >= 0) & (j < count))
        def _():
            at, slot = rows_of(j), slot_of(j)

            @pl.when(first)
            def _():
                held[slot, :] = own[at, :]

            @pl.when(jnp.logical_not(first))
            def _():
                make(j).wait_recv()
                held[slot, :] = held[slot, :] + own[at, :]

            @pl.when(jnp.logical_not(last))
            def _():
                send(make, j)

    settle = HOP * jnp.maximum(l, loops - 1 - l)

    def multiply(g, n):
        at = pl.ds(pl.multiple_of(g * span, span), span)

        @pl.when(n == 0)
        def _():
            @pl.loop(0, mrows // 256)
            def _(m):
                mine = pl.ds(pl.multiple_of(m * 256, 256), 256)
                high, low = split(own[at, mine].T)
                left[mine, pl.ds(0, span)] = high
                left[mine, pl.ds(span, span)] = high
                left[mine, pl.ds(2 * span, span)] = low

        @pl.when(n < 2 * (mrows // 256))
        def _():
            block = n // (mrows // 256)
            inner = pl.multiple_of(lax.rem(n, mrows // 256) * 256, 256)
            high, low = split(cols[block, at, pl.ds(inner, 256)])
            right = jnp.concatenate([high, low, high], axis=0)
            theirs = pl.ds(pl.multiple_of(n * 256, 256), 256)

            @pl.loop(0, mrows // 256)
            def _(m):
                mine = pl.ds(pl.multiple_of(m * 256, 256), 256)
                part = jnp.dot(left[mine, :], right, preferred_element_type=jnp.float32) * scale

                @pl.when(g == 0)
                def _():
                    out_ref[mine, theirs] = part

                @pl.when(g > 0)
                def _():
                    out_ref[mine, theirs] = out_ref[mine, theirs] + part

    def step(t, carry):
        line(pin, up, t - HOP * l, l == 0, l == loops - 1)
        line(sin, down, t - HOP * (loops - 1 - l), l == loops - 1, l == 0)

        done = t - settle

        @pl.when((done >= 0) & (done < count))
        def _():
            at, slot = rows_of(done), slot_of(done)
            total = pin[slot, :] + (sin[slot, :] - own[at, :])
            own[at, :] = total

            @pl.when(far == 0)
            def _():
                cols[core, at, :] = total

        passed = done - REACH * far

        @pl.when((passed >= 0) & (passed < count))
        def _():
            @pl.when(far > 0)
            def _():
                chain(passed).wait_recv()

            @pl.when(far < pairs - 1)
            def _():
                send(chain, passed)

            send(share, passed)

        ready = done - REACH * pairs

        @pl.when((ready >= 0) & (ready < count))
        def _():
            taken(ready).wait_recv()

        @pl.when((ready >= GROUP) & (ready < count + GROUP))
        def _():
            multiply(ready // GROUP - 1, lax.rem(ready, GROUP))

        later = tiles + t // pace

        @pl.when((lax.rem(t, pace) == pace // 2) & (later < tile_count))
        def _():
            half(later)

        return carry

    lax.fori_loop(0, count + HOP * (loops - 1) + REACH * pairs + GROUP, step, 0)

    def drain(i, carry):
        j = count - SLOTS + i

        @pl.when(l < loops - 1)
        def _():
            up(j).wait_send()

        @pl.when(l > 0)
        def _():
            down(j).wait_send()

        @pl.when(far < pairs - 1)
        def _():
            chain(j).wait_send()

        share(j).wait_send()
        return carry

    lax.fori_loop(0, SLOTS, drain, 0)


def local(loops, row_count, integrals, mask, coeffs):
    nslab, naux, mrows, lcols = integrals.shape
    norbit = coeffs.shape[1]
    depth = nslab * naux * norbit
    count = depth // CHUNK
    wide = 2 * TILE
    assert lcols == 2 * mrows and row_count == 2 * loops and norbit % CHUNK == 0
    assert depth % (CHUNK * GROUP) == 0 and 2 * mrows // 256 <= GROUP
    ring = min(count, SLOTS + 3 * HOP * loops)
    spare = (8, 128) if lcols <= depth and norbit <= mrows else (lcols, norbit)
    blocks = jnp.repeat(mask.astype(jnp.float32), TILE, axis=2)
    blocks = blocks.reshape(nslab, mrows // wide, wide // TILE, lcols)
    dma = pltpu.SemaphoreType.DMA
    return pl.pallas_call(
        functools.partial(exchange_kernel, loops, row_count, float(depth) ** -0.5),
        out_shape=jax.ShapeDtypeStruct((mrows, lcols), jnp.float32),
        in_specs=[
            pl.BlockSpec(memory_space=pl.ANY),
            pl.BlockSpec(memory_space=pltpu.VMEM),
            pl.BlockSpec(memory_space=pl.ANY),
        ],
        out_specs=pl.BlockSpec(memory_space=pltpu.VMEM),
        scratch_shapes=[
            pltpu.VMEM((depth, mrows), jnp.float32),
            pltpu.VMEM((ring * CHUNK, mrows), jnp.float32),
            pltpu.VMEM((ring * CHUNK, mrows), jnp.float32),
            pltpu.VMEM((2, depth, mrows), jnp.float32),
            pltpu.VMEM((mrows, 3 * CHUNK * GROUP), jnp.bfloat16),
            pltpu.VMEM((norbit, lcols), jnp.bfloat16),
            pltpu.VMEM((norbit, lcols), jnp.bfloat16),
            pltpu.VMEM((2, wide, lcols), jnp.float32),
            pltpu.VMEM(spare, jnp.float32),
            dma((2,)),
            dma,
        ]
        + [dma((SLOTS,)), dma((count,))] * 4,
        compiler_params=pltpu.CompilerParams(
            collective_id=0, has_side_effects=True, vmem_limit_bytes=67043328
        ),
        name="exchange",
    )(integrals, blocks, coeffs)


def solution(mesh):
    in_specs = (P(None, None, "rows", "loop"), P(None, "rows", "loop"), P("loop", None))
    out_specs = P("rows", "loop")
    body = functools.partial(local, mesh.shape["loop"], mesh.shape["rows"])
    return jax.shard_map(body, mesh=mesh, in_specs=in_specs, out_specs=out_specs, check_vma=False)
```
